512 devices in a mesh: grp: 16 (over z), row: 32 (over x, y, core).
Axes of the slice: x: 4, y: 4, z: 16, core: 2. Of those that a mesh axis runs over, the one named last changes fastest.
Arguments:
- design: bfloat16 [786432, 512], P(('grp', 'row')), may hold values from -0.29882812 to 0.29882812
- scales: bfloat16 [786432], P(('grp', 'row')), may hold values from 0.3984375 to 9.5
- buckets: int32 [786432], P(('grp', 'row')), may hold values from 0 to 1535
Outputs:
- sketch: float32 [24576, 512], P(('grp', 'row'))
- precond: float32 [512, 512], P('grp')
The draws below stay inside these ranges and needn't reach their ends.
All inputs are finite; a program needn't handle non-finite values.
Results may differ from the reference program's by a relative error of at most 0.0003.
Values sent between devices are 32-bit elements; how exact they have to be, the bound alone decides.
No kernel may reach another device: no remote copies, remote signals or barrier semaphores. Data moves between devices by JAX's collectives and lax.ppermute only.
A program may use at most 64 MiB of HBM per device.

```python
import math
import jax
import jax.numpy as jnp
from jax import lax

D = 512
ROWS_DEV = 1536
ROWS = 786432
N_GRP = 16
N_ROW = 32


def place_ends(entries, own_key, least, largest):
    spot = [jax.random.randint(jax.random.fold_in(own_key, axis), (), 0, length) for axis, length in enumerate(entries.shape)]
    longest = entries.shape.index(max(entries.shape))
    next_to = spot[:longest] + [(spot[longest] + 1) % entries.shape[longest]] + spot[longest + 1:]
    return entries.at[tuple(spot)].set(least).at[tuple(next_to)].set(largest)


def block_levels(stream_key, extent, shards, least, top_value):
    def one(position, blocks):
        steps = jax.random.uniform(jax.random.fold_in(jax.random.fold_in(stream_key, 6), position), (blocks,), jnp.float32, least / len(shards), top_value / len(shards))
        return jnp.repeat(jnp.exp(steps), extent[position] // blocks).reshape((-1,) + (1,) * (len(extent) - position - 1))

    factor_of = one(*shards[0])
    for cut in shards[1:]:
        factor_of = factor_of * one(*cut)
    return factor_of


def scatter_about(rng, shape, deviation, most, split=(), kind=jnp.bfloat16):
    result = jax.random.normal(rng, shape, jnp.float32) * deviation
    if len(split) > 0:
        result = block_levels(rng, shape, split, -0.22, 0.18) * result
    return jnp.clip(result, min=-most, max=most).astype(kind)


def setup_inputs(seed: int = 0) -> dict:
    splits = jax.random.split(jax.random.key(seed), 4)
    return {
        "design": scatter_about(splits[0], (ROWS, D), 0.05, 0.29882812, ((0, 512),)),
        "scales": jnp.clip(jnp.exp(math.log(9.5) - 3.1714964 * jax.random.uniform(splits[1], (ROWS,), jnp.float32) ** block_levels(splits[1], (ROWS,), ((0, 512),), -0.2, 0.2)), 0.3984375, 9.5).astype(jnp.bfloat16),
        "buckets": place_ends(jax.random.randint(splits[2], (ROWS,), 0, ROWS_DEV), jax.random.fold_in(splits[2], 1), 0, ROWS_DEV - 1).astype(jnp.int32),
    }


def embed_group(pieces):
    rows_blk, weights, bucket_ids = pieces
    weighted = rows_blk.astype(jnp.float32) * weights.astype(jnp.float32)[:, None]
    return jax.ops.segment_sum(weighted, bucket_ids, num_segments=ROWS_DEV)

def reference(design, scales, buckets):
    per_group = ROWS_DEV * N_ROW
    grouped = (design.reshape(N_GRP, per_group, D), scales.reshape(N_GRP, per_group), buckets.reshape(N_GRP, per_group))
    sketch = lax.map(embed_group, grouped).reshape(N_GRP * ROWS_DEV, D)
    gram_matrix = jnp.dot(sketch.T.astype(jnp.float32), sketch.astype(jnp.float32), precision=lax.Precision.HIGHEST, preferred_element_type=jnp.float32)
    factor = jnp.linalg.cholesky(gram_matrix).T
    precond = factor / jnp.sqrt(jnp.float32(N_GRP * ROWS_DEV))
    return (sketch, precond)
```

```python
import jax
import jax.numpy as jnp
from jax import lax
from jax.sharding import Mesh
from jax.sharding import PartitionSpec as P

TILE = 128
ALL = ("zh", "zl", "x", "y", "core")


def blocks_of(size):
    count = size // TILE
    return [(i, j) for i in range(count) for j in range(i, count)]


def exchange(value, axes):
    return lax.all_to_all(value, axes, split_axis=0, concat_axis=0, tiled=True)


def spread(value, axes):
    count = lax.axis_size(axes)
    return exchange(jnp.broadcast_to(value[None], (count,) + value.shape), axes)


def self_gram(matrix):
    return lax.dot_general(
        matrix,
        matrix,
        (((0,), (0,)), ((), ())),
        precision=lax.Precision.HIGHEST,
        preferred_element_type=jnp.float32,
    )


def bucket_sums(design, scales, buckets, core, chips, owned):
    slots = lax.broadcasted_iota(jnp.int32, (chips, owned), 0) * (2 * owned) + core * owned
    slots = (slots + lax.broadcasted_iota(jnp.int32, (chips, owned), 1)).reshape(-1)
    table = jnp.where(slots[:, None] == buckets[None, :], scales[None, :], jnp.zeros((), jnp.bfloat16))
    return jnp.dot(table, design, preferred_element_type=jnp.float32)


def per_device(design, scales, buckets):
    rows, cols = design.shape
    chips = lax.axis_size(("x", "y"))
    owned = rows // (2 * chips)
    core = lax.axis_index("core")
    theirs = bucket_sums(design, scales, buckets, 1 - core, chips, owned)
    from_pair = lax.ppermute(theirs, "core", [(0, 1), (1, 0)])
    ours = bucket_sums(design, scales, buckets, core, chips, owned)
    paired = (ours + from_pair).reshape(chips, owned, cols)
    sketch = jnp.sum(exchange(paired, ("x", "y")), axis=0)
    local = self_gram(sketch)
    pairs = blocks_of(cols)
    packed = jnp.stack(
        [local[i * TILE : (i + 1) * TILE, j * TILE : (j + 1) * TILE] for i, j in pairs]
    )
    devices = 2 * chips
    packed = packed.reshape(devices, -1, TILE)
    piece = jnp.sum(exchange(packed, ("x", "y", "core")), axis=0)
    piece = jnp.sum(spread(piece, ("zl",)), axis=0)
    piece = jnp.sum(spread(piece, ("zh",)), axis=0)
    whole = spread(piece, ("x", "y", "core")).reshape(len(pairs), TILE, TILE)
    at = {pair: n for n, pair in enumerate(pairs)}
    count = cols // TILE
    gram = jnp.concatenate(
        [
            jnp.concatenate(
                [whole[at[i, j]] if i <= j else whole[at[j, i]].T for j in range(count)], axis=1
            )
            for i in range(count)
        ],
        axis=0,
    )
    groups = lax.axis_size(("zh", "zl"))
    precond = jnp.linalg.cholesky(gram, symmetrize_input=False).T / jnp.sqrt(jnp.float32(rows * groups))
    slab = cols // groups
    start = lax.axis_index(("zh", "zl")) * slab
    return sketch, lax.dynamic_slice_in_dim(precond, start, slab, 0)


def solution(mesh):
    fine = Mesh(mesh.devices.reshape(4, 4, 4, 4, 2), ALL)
    rows = ALL
    in_specs = (P(rows, None), P(rows), P(rows))
    out_specs = (P(rows, None), P(("zh", "zl"), None))
    return jax.shard_map(
        per_device, mesh=fine, in_specs=in_specs, out_specs=out_specs, check_vma=False
    )
```

```python
import functools
import math

import jax
import jax.numpy as jnp
from jax import lax
from jax.experimental import pallas as pl
from jax.experimental.pallas import tpu as pltpu
from jax.sharding import Mesh
from jax.sharding import PartitionSpec as P

TILE = 128
SUB = 8
ALL = ("zh", "zl", "x", "y", "core")


def blocks_of(size):
    count = size // TILE
    return [(i, j) for i in range(count) for j in range(i, count)]


def exchange(value, axes):
    return lax.all_to_all(value, axes, split_axis=0, concat_axis=0, tiled=True)


def spread(value, axes):
    count = lax.axis_size(axes)
    return exchange(jnp.broadcast_to(value[None], (count,) + value.shape), axes)


def self_gram(matrix):
    return lax.dot_general(
        matrix,
        matrix,
        (((0,), (0,)), ((), ())),
        precision=lax.Precision.HIGHEST,
        preferred_element_type=jnp.float32,
    )


def bucket_sums(design, scales, buckets, core, chips, owned):
    slots = lax.broadcasted_iota(jnp.int32, (chips, owned), 0) * (2 * owned) + core * owned
    slots = (slots + lax.broadcasted_iota(jnp.int32, (chips, owned), 1)).reshape(-1)
    table = jnp.where(slots[:, None] == buckets[None, :], scales[None, :], jnp.zeros((), jnp.bfloat16))
    return jnp.dot(table, design, preferred_element_type=jnp.float32)


def terms(value):
    high = value.astype(jnp.bfloat16).astype(jnp.float32)
    rest = value - high
    middle = rest.astype(jnp.bfloat16).astype(jnp.float32)
    return high, middle, rest - middle


def rank_update(left, right):
    a, b, c = terms(left)
    d, e, f = terms(right)
    tall = jnp.concatenate([a, a, b, b, a, c], 0).astype(jnp.bfloat16)
    wide = jnp.concatenate([d, e, d, e, f, d], 0).astype(jnp.bfloat16)
    return lax.dot_general(tall, wide, (((0,), (0,)), ((), ())), preferred_element_type=jnp.float32)


def fill(value):
    return jnp.broadcast_to(value, (SUB, TILE))


def factor_kernel(slab_ref, gram_ref, out_ref, work, *, count, scale):
    at = {pair: n for n, pair in enumerate(blocks_of(count * TILE))}
    work[...] = gram_ref[...]
    for b in range(count):
        js = range(b, count)
        ahead = None
        for top in range(0, TILE, SUB):
            rows = ahead
            if rows is None:
                rows = [{j: fill(work[at[b, j], top + t : top + t + 1, :]) for j in js} for t in range(SUB)]
            pivot = {
                (t, u): fill(rows[t][b][:, top + u : top + u + 1]) for t in range(SUB) for u in range(t, SUB)
            }
            done = []
            for t in range(SUB):
                inverse = lax.rsqrt(pivot[t, t])
                coef = {u: pivot[t, u] * inverse for u in range(t + 1, SUB)}
                for u in range(t + 1, SUB):
                    for v in range(u, SUB):
                        pivot[u, v] = pivot[u, v] - coef[u] * coef[v]
                done.append({j: rows[t][j] * inverse for j in js})
                for u in range(t + 1, SUB):
                    for j in js:
                        rows[u][j] = rows[u][j] - coef[u] * done[t][j]
            for t in range(SUB):
                for j in js:
                    work[at[b, j], top + t : top + t + 1, :] = done[t][j][0:1, :]
            ahead = None
            below = top + SUB
            if below < TILE:
                ahead = [
                    {j: fill(work[at[b, j], below + u : below + u + 1, :]) for j in js} for u in range(SUB)
                ]
                for t in range(SUB):
                    for u in range(SUB):
                        coef = fill(done[t][b][:, below + u : below + u + 1])
                        for j in js:
                            ahead[u][j] = ahead[u][j] - coef * done[t][j]
            later = top + 2 * SUB
            if later < TILE:
                left = work[at[b, b], top : top + SUB, :]
                for j in js:
                    update = rank_update(left, work[at[b, j], top : top + SUB, :])
                    work[at[b, j], later:, :] = work[at[b, j], later:, :] - update[later:, :]
        for i in range(b + 1, count):
            for j in range(i, count):
                work[at[i, j]] = work[at[i, j]] - lax.dot_general(
                    work[at[b, i]],
                    work[at[b, j]],
                    (((0,), (0,)), ((), ())),
                    precision=lax.Precision.HIGHEST,
                    preferred_element_type=jnp.float32,
                )
    slab = slab_ref[0]
    height = out_ref.shape[0]
    per_tile = TILE // height
    for i in range(count):

        @pl.when(slab // per_tile == i)
        def _():
            start = pl.multiple_of((slab % per_tile) * height, height)
            shape = (height, TILE)
            for j in range(count):
                if j < i:
                    value = jnp.zeros(shape, jnp.float32)
                else:
                    value = work[at[i, j], pl.ds(start, height), :] * scale
                if j == i:
                    upper = lax.broadcasted_iota(jnp.int32, shape, 1) >= start + lax.broadcasted_iota(
                        jnp.int32, shape, 0
                    )
                    value = jnp.where(upper, value, 0.0)
                out_ref[:, j * TILE : (j + 1) * TILE] = value


def factor_rows(slab, packed, height, cols, scale):
    return pl.pallas_call(
        functools.partial(factor_kernel, count=cols // TILE, scale=scale),
        out_shape=jax.ShapeDtypeStruct((height, cols), jnp.float32),
        in_specs=[pl.BlockSpec(memory_space=pltpu.SMEM), pl.BlockSpec(memory_space=pltpu.VMEM)],
        out_specs=pl.BlockSpec(memory_space=pltpu.VMEM),
        scratch_shapes=[pltpu.VMEM(packed.shape, jnp.float32)],
        name="factor_rows",
    )(slab.reshape(1), packed)


def per_device(design, scales, buckets):
    rows, cols = design.shape
    chips = lax.axis_size(("x", "y"))
    owned = rows // (2 * chips)
    core = lax.axis_index("core")
    theirs = bucket_sums(design, scales, buckets, 1 - core, chips, owned)
    from_pair = lax.ppermute(theirs, "core", [(0, 1), (1, 0)])
    ours = bucket_sums(design, scales, buckets, core, chips, owned)
    paired = (ours + from_pair).reshape(chips, owned, cols)
    sketch = jnp.sum(exchange(paired, ("x", "y")), axis=0)
    local = self_gram(sketch)
    pairs = blocks_of(cols)
    packed = jnp.stack(
        [local[i * TILE : (i + 1) * TILE, j * TILE : (j + 1) * TILE] for i, j in pairs]
    )
    devices = 2 * chips
    packed = packed.reshape(devices, -1, TILE)
    piece = jnp.sum(exchange(packed, ("x", "y", "core")), axis=0)
    piece = jnp.sum(spread(piece, ("zl",)), axis=0)
    piece = jnp.sum(spread(piece, ("zh",)), axis=0)
    whole = spread(piece, ("x", "y", "core")).reshape(len(pairs), TILE, TILE)
    groups = lax.axis_size(("zh", "zl"))
    slab = lax.axis_index(("zh", "zl")).astype(jnp.int32)
    precond = factor_rows(slab, whole, cols // groups, cols, 1.0 / math.sqrt(rows * groups))
    return sketch, precond


def solution(mesh):
    fine = Mesh(mesh.devices.reshape(4, 4, 4, 4, 2), ALL)
    rows = ALL
    in_specs = (P(rows, None), P(rows), P(rows))
    out_specs = (P(rows, None), P(("zh", "zl"), None))
    return jax.shard_map(
        per_device, mesh=fine, in_specs=in_specs, out_specs=out_specs, check_vma=False
    )
```

```python
import functools
import math

import jax
import jax.numpy as jnp
from jax import lax
from jax.experimental import pallas as pl
from jax.experimental.pallas import tpu as pltpu
from jax.sharding import Mesh
from jax.sharding import PartitionSpec as P

TILE = 128
SUB = 8
ALL = ("zh", "zl", "x", "y", "core")


def blocks_of(size):
    count = size // TILE
    return [(i, j) for i in range(count) for j in range(i, count)]


def exchange(value, axes):
    return lax.all_to_all(value, axes, split_axis=0, concat_axis=0, tiled=True)


def spread(value, axes):
    count = lax.axis_size(axes)
    return exchange(jnp.broadcast_to(value[None], (count,) + value.shape), axes)


def self_gram(matrix):
    return lax.dot_general(
        matrix,
        matrix,
        (((0,), (0,)), ((), ())),
        precision=lax.Precision.HIGHEST,
        preferred_element_type=jnp.float32,
    )


def bucket_sums(design, scales, buckets, core, chips, owned):
    slots = lax.broadcasted_iota(jnp.int32, (chips, owned), 0) * (2 * owned) + core * owned
    slots = (slots + lax.broadcasted_iota(jnp.int32, (chips, owned), 1)).reshape(-1)
    table = jnp.where(slots[:, None] == buckets[None, :], scales[None, :], jnp.zeros((), jnp.bfloat16))
    return jnp.dot(table, design, preferred_element_type=jnp.float32)


def terms(value):
    high = value.astype(jnp.bfloat16).astype(jnp.float32)
    rest = value - high
    middle = rest.astype(jnp.bfloat16).astype(jnp.float32)
    return high, middle, rest - middle


def rank_update(left, right):
    a, b, c = terms(left)
    d, e, f = terms(right)
    tall = jnp.concatenate([a, a, b, b, a, c], 0).astype(jnp.bfloat16)
    wide = jnp.concatenate([d, e, d, e, f, d], 0).astype(jnp.bfloat16)
    return lax.dot_general(tall, wide, (((0,), (0,)), ((), ())), preferred_element_type=jnp.float32)


def fill(value):
    return jnp.broadcast_to(value, (SUB, TILE))


def pivots_of(rows, left):
    return {(t, u): fill(rows[t][:, left + u : left + u + 1]) for t in range(SUB) for u in range(t, SUB)}


def factor_kernel(slab_ref, gram_ref, out_ref, work, *, count, scale):
    at = {pair: n for n, pair in enumerate(blocks_of(count * TILE))}
    work[...] = gram_ref[...]
    for b in range(count):
        js = range(b, count)
        ahead = ready = None
        for top in range(0, TILE, SUB):
            rows, pivot = ahead, ready
            if rows is None:
                rows = [{j: fill(work[at[b, j], top + t : top + t + 1, :]) for j in js} for t in range(SUB)]
                pivot = pivots_of([row[b] for row in rows], top)
            done = []
            for t in range(SUB):
                inverse = lax.rsqrt(pivot[t, t])
                coef = {u: pivot[t, u] * inverse for u in range(t + 1, SUB)}
                for u in range(t + 1, SUB):
                    for v in range(u, SUB):
                        pivot[u, v] = pivot[u, v] - coef[u] * coef[v]
                done.append({j: rows[t][j] * inverse for j in js})
                for u in range(t + 1, SUB):
                    for j in js:
                        rows[u][j] = rows[u][j] - coef[u] * done[t][j]
            for t in range(SUB):
                for j in js:
                    work[at[b, j], top + t : top + t + 1, :] = done[t][j][0:1, :]
            ahead = ready = None
            below = top + SUB
            if below < TILE:
                ahead = [
                    {j: fill(work[at[b, j], below + u : below + u + 1, :]) for j in js} for u in range(SUB)
                ]
                for t in range(SUB):
                    if t == SUB // 2:
                        ready = pivots_of([row[b] for row in ahead], below)
                    coef = [fill(done[t][b][:, below + u : below + u + 1]) for u in range(SUB)]
                    if ready is not None:
                        for u, v in ready:
                            ready[u, v] = ready[u, v] - coef[u] * coef[v]
                    for u in range(SUB):
                        for j in js:
                            ahead[u][j] = ahead[u][j] - coef[u] * done[t][j]
            later = top + 2 * SUB
            if later < TILE:
                left = work[at[b, b], top : top + SUB, :]
                for j in js:
                    update = rank_update(left, work[at[b, j], top : top + SUB, :])
                    work[at[b, j], later:, :] = work[at[b, j], later:, :] - update[later:, :]
        for i in range(b + 1, count):
            for j in range(i, count):
                work[at[i, j]] = work[at[i, j]] - lax.dot_general(
                    work[at[b, i]],
                    work[at[b, j]],
                    (((0,), (0,)), ((), ())),
                    precision=lax.Precision.HIGHEST,
                    preferred_element_type=jnp.float32,
                )
    slab = slab_ref[0]
    height = out_ref.shape[0]
    per_tile = TILE // height
    for i in range(count):

        @pl.when(slab // per_tile == i)
        def _():
            start = pl.multiple_of((slab % per_tile) * height, height)
            shape = (height, TILE)
            for j in range(count):
                if j < i:
                    value = jnp.zeros(shape, jnp.float32)
                else:
                    value = work[at[i, j], pl.ds(start, height), :] * scale
                if j == i:
                    upper = lax.broadcasted_iota(jnp.int32, shape, 1) >= start + lax.broadcasted_iota(
                        jnp.int32, shape, 0
                    )
                    value = jnp.where(upper, value, 0.0)
                out_ref[:, j * TILE : (j + 1) * TILE] = value


def factor_rows(slab, packed, height, cols, scale):
    return pl.pallas_call(
        functools.partial(factor_kernel, count=cols // TILE, scale=scale),
        out_shape=jax.ShapeDtypeStruct((height, cols), jnp.float32),
        in_specs=[pl.BlockSpec(memory_space=pltpu.SMEM), pl.BlockSpec(memory_space=pltpu.VMEM)],
        out_specs=pl.BlockSpec(memory_space=pltpu.VMEM),
        scratch_shapes=[pltpu.VMEM(packed.shape, jnp.float32)],
        name="factor_rows",
    )(slab.reshape(1), pltpu.with_memory_space_constraint(packed, pltpu.VMEM))


def per_device(design, scales, buckets):
    rows, cols = design.shape
    chips = lax.axis_size(("x", "y"))
    owned = rows // (2 * chips)
    core = lax.axis_index("core")
    slab = lax.axis_index(("zh", "zl")).astype(jnp.int32)
    core, slab, buckets = lax.optimization_barrier((core, slab, buckets))
    theirs = bucket_sums(design, scales, buckets, 1 - core, chips, owned)
    from_pair = lax.ppermute(theirs, "core", [(0, 1), (1, 0)])
    ours = lax.optimization_barrier(bucket_sums(design, scales, buckets, core, chips, owned))
    paired = (ours + from_pair).reshape(chips, owned, cols)
    sketch = jnp.sum(exchange(paired, ("x", "y")), axis=0)
    local = self_gram(sketch)
    pairs = blocks_of(cols)
    packed = jnp.stack(
        [local[i * TILE : (i + 1) * TILE, j * TILE : (j + 1) * TILE] for i, j in pairs]
    )
    devices = 2 * chips
    packed = packed.reshape(devices, -1, TILE)
    piece = jnp.sum(exchange(packed, ("x", "y", "core")), axis=0)
    piece = jnp.sum(spread(piece, ("zh",)), axis=0)
    piece = jnp.sum(spread(piece, ("zl",)), axis=0)
    whole = spread(piece, ("x", "y", "core")).reshape(len(pairs), TILE, TILE)
    groups = lax.axis_size(("zh", "zl"))
    precond = factor_rows(slab, whole, cols // groups, cols, 1.0 / math.sqrt(rows * groups))
    return sketch, precond


def solution(mesh):
    fine = Mesh(mesh.devices.reshape(4, 4, 4, 4, 2), ALL)
    rows = ALL
    in_specs = (P(rows, None), P(rows), P(rows))
    out_specs = (P(rows, None), P(("zh", "zl"), None))
    return jax.shard_map(
        per_device, mesh=fine, in_specs=in_specs, out_specs=out_specs, check_vma=False
    )
```

```python
import functools
import math

import jax
import jax.numpy as jnp
from jax import lax
from jax.experimental import pallas as pl
from jax.experimental.pallas import tpu as pltpu
from jax.sharding import Mesh
from jax.sharding import PartitionSpec as P

TILE = 128
SUB = 8
ALL = ("zh", "zl", "x", "y", "core")


def blocks_of(size):
    count = size // TILE
    return [(i, j) for i in range(count) for j in range(i, count)]


def folded_of(size):
    count = size // TILE
    return [(i, i + 1) for i in range(0, count, 2)], [(i, j) for i in range(count) for j in range(i + 1, count)]


def fold(gram, squares, devices):
    block = lambda i, j: gram[i * TILE : (i + 1) * TILE, j * TILE : (j + 1) * TILE]
    rows, lanes = (lax.broadcasted_iota(jnp.int32, (TILE, TILE), d) for d in (0, 1))
    pairs, above = folded_of(gram.shape[0])
    parts = [jnp.where(rows <= lanes, block(i, i), block(j, j)) for i, j in pairs]
    parts += [block(i, j) for i, j in above]
    parts += [squares[j * TILE : (j + 1) * TILE][None] for _, j in pairs]
    height = sum(part.shape[0] for part in parts)
    missing = -height % devices
    parts.append(jnp.zeros((missing, TILE), jnp.float32))
    return jnp.concatenate(parts, axis=0).reshape(devices, (height + missing) // devices, 1, TILE)


def exchange(value, axes):
    return lax.all_to_all(value, axes, split_axis=0, concat_axis=0, tiled=True)


def spread(value, axes):
    count = lax.axis_size(axes)
    return exchange(jnp.broadcast_to(value[None], (count,) + value.shape), axes)


def self_gram(matrix):
    return lax.dot_general(
        matrix,
        matrix,
        (((0,), (0,)), ((), ())),
        precision=lax.Precision.HIGHEST,
        preferred_element_type=jnp.float32,
    )


def bucket_sums(design, scales, buckets, core, chips, owned):
    slots = lax.broadcasted_iota(jnp.int32, (chips, owned), 0) * (2 * owned) + core * owned
    slots = (slots + lax.broadcasted_iota(jnp.int32, (chips, owned), 1)).reshape(-1)
    table = jnp.where(slots[:, None] == buckets[None, :], scales[None, :], jnp.zeros((), jnp.bfloat16))
    return jnp.dot(table, design, preferred_element_type=jnp.float32)


def terms(value):
    high = value.astype(jnp.bfloat16).astype(jnp.float32)
    rest = value - high
    middle = rest.astype(jnp.bfloat16).astype(jnp.float32)
    return high, middle, rest - middle


def rank_update(left, right):
    a, b, c = terms(left)
    d, e, f = terms(right)
    tall = jnp.concatenate([a, a, b, b, a, c], 0).astype(jnp.bfloat16)
    wide = jnp.concatenate([d, e, d, e, f, d], 0).astype(jnp.bfloat16)
    return lax.dot_general(tall, wide, (((0,), (0,)), ((), ())), preferred_element_type=jnp.float32)


def fill(value):
    return jnp.broadcast_to(value, (SUB, TILE))


def pivots_of(rows, left):
    return {(t, u): fill(rows[t][:, left + u : left + u + 1]) for t in range(SUB) for u in range(t, SUB)}


def factor_kernel(slab_ref, gram_ref, out_ref, work, *, count, scale):
    at = {pair: n for n, pair in enumerate(blocks_of(count * TILE))}
    pairs, above = folded_of(count * TILE)
    shape = (TILE, TILE)
    rows, lanes = lax.broadcasted_iota(jnp.int32, shape, 0), lax.broadcasted_iota(jnp.int32, shape, 1)
    last = (len(pairs) + len(above)) * TILE
    for n, (i, j) in enumerate(pairs):
        both = gram_ref[n * TILE : (n + 1) * TILE, :]
        work[at[i, i]] = both
        diagonal = jnp.broadcast_to(gram_ref[last + n : last + n + 1, :], shape)
        work[at[j, j]] = jnp.where(rows == lanes, diagonal, both.T)
    for n, pair in enumerate(above, len(pairs)):
        work[at[pair]] = gram_ref[n * TILE : (n + 1) * TILE, :]
    for b in range(count):
        js = range(b, count)
        ahead = ready = None
        for top in range(0, TILE, SUB):
            rows, pivot = ahead, ready
            if rows is None:
                rows = [{j: fill(work[at[b, j], top + t : top + t + 1, :]) for j in js} for t in range(SUB)]
                pivot = pivots_of([row[b] for row in rows], top)
            done = []
            for t in range(SUB):
                inverse = lax.rsqrt(pivot[t, t])
                coef = {u: pivot[t, u] * inverse for u in range(t + 1, SUB)}
                for u in range(t + 1, SUB):
                    for v in range(u, SUB):
                        pivot[u, v] = pivot[u, v] - coef[u] * coef[v]
                done.append({j: rows[t][j] * inverse for j in js})
                for u in range(t + 1, SUB):
                    for j in js:
                        rows[u][j] = rows[u][j] - coef[u] * done[t][j]
            for t in range(SUB):
                for j in js:
                    work[at[b, j], top + t : top + t + 1, :] = done[t][j][0:1, :]
            ahead = ready = None
            below = top + SUB
            if below < TILE:
                ahead = [
                    {j: fill(work[at[b, j], below + u : below + u + 1, :]) for j in js} for u in range(SUB)
                ]
                for t in range(SUB):
                    if t == SUB // 2:
                        ready = pivots_of([row[b] for row in ahead], below)
                    coef = [fill(done[t][b][:, below + u : below + u + 1]) for u in range(SUB)]
                    if ready is not None:
                        for u, v in ready:
                            ready[u, v] = ready[u, v] - coef[u] * coef[v]
                    for u in range(SUB):
                        for j in js:
                            ahead[u][j] = ahead[u][j] - coef[u] * done[t][j]
            later = top + 2 * SUB
            if later < TILE:
                left = work[at[b, b], top : top + SUB, :]
                for j in js:
                    update = rank_update(left, work[at[b, j], top : top + SUB, :])
                    work[at[b, j], later:, :] = work[at[b, j], later:, :] - update[later:, :]
        for i in range(b + 1, count):
            for j in range(i, count):
                work[at[i, j]] = work[at[i, j]] - lax.dot_general(
                    work[at[b, i]],
                    work[at[b, j]],
                    (((0,), (0,)), ((), ())),
                    precision=lax.Precision.HIGHEST,
                    preferred_element_type=jnp.float32,
                )
    slab = slab_ref[0]
    height = out_ref.shape[0]
    per_tile = TILE // height
    for i in range(count):

        @pl.when(slab // per_tile == i)
        def _():
            start = pl.multiple_of((slab % per_tile) * height, height)
            shape = (height, TILE)
            for j in range(count):
                if j < i:
                    value = jnp.zeros(shape, jnp.float32)
                else:
                    value = work[at[i, j], pl.ds(start, height), :] * scale
                if j == i:
                    upper = lax.broadcasted_iota(jnp.int32, shape, 1) >= start + lax.broadcasted_iota(
                        jnp.int32, shape, 0
                    )
                    value = jnp.where(upper, value, 0.0)
                out_ref[:, j * TILE : (j + 1) * TILE] = value


def factor_rows(slab, packed, height, cols, scale):
    return pl.pallas_call(
        functools.partial(factor_kernel, count=cols // TILE, scale=scale),
        out_shape=jax.ShapeDtypeStruct((height, cols), jnp.float32),
        in_specs=[pl.BlockSpec(memory_space=pltpu.SMEM), pl.BlockSpec(memory_space=pltpu.VMEM)],
        out_specs=pl.BlockSpec(memory_space=pltpu.VMEM),
        scratch_shapes=[pltpu.VMEM((len(blocks_of(cols)), TILE, TILE), jnp.float32)],
        name="factor_rows",
    )(slab.reshape(1), pltpu.with_memory_space_constraint(packed, pltpu.VMEM))


def per_device(design, scales, buckets):
    rows, cols = design.shape
    chips = lax.axis_size(("x", "y"))
    owned = rows // (2 * chips)
    core = lax.axis_index("core")
    slab = lax.axis_index(("zh", "zl")).astype(jnp.int32)
    core, slab, buckets = lax.optimization_barrier((core, slab, buckets))
    theirs = bucket_sums(design, scales, buckets, 1 - core, chips, owned)
    from_pair = lax.ppermute(theirs, "core", [(0, 1), (1, 0)])
    ours = lax.optimization_barrier(bucket_sums(design, scales, buckets, core, chips, owned))
    paired = (ours + from_pair).reshape(chips, owned, cols)
    sketch = jnp.sum(exchange(paired, ("x", "y")), axis=0)
    local = self_gram(sketch)
    packed = fold(local, jnp.sum(sketch * sketch, axis=0), 2 * chips)
    piece = jnp.sum(exchange(packed, ("x", "y", "core")), axis=0)
    piece = jnp.sum(spread(piece, ("zh",)), axis=0)
    piece = jnp.sum(spread(piece, ("zl",)), axis=0)
    whole = spread(piece, ("x", "y", "core")).reshape(-1, TILE)
    groups = lax.axis_size(("zh", "zl"))
    precond = factor_rows(slab, whole, cols // groups, cols, 1.0 / math.sqrt(rows * groups))
    return sketch, precond


def solution(mesh):
    fine = Mesh(mesh.devices.reshape(4, 4, 4, 4, 2), ALL)
    rows = ALL
    in_specs = (P(rows, None), P(rows), P(rows))
    out_specs = (P(rows, None), P(("zh", "zl"), None))
    return jax.shard_map(
        per_device, mesh=fine, in_specs=in_specs, out_specs=out_specs, check_vma=False
    )
```

```python
import functools
import math

import jax
import jax.numpy as jnp
from jax import lax
from jax.experimental import pallas as pl
from jax.experimental.pallas import tpu as pltpu
from jax.sharding import Mesh
from jax.sharding import PartitionSpec as P

TILE = 128
SUB = 8
ALL = ("zh", "zl", "x", "y", "core")


def blocks_of(size):
    count = size // TILE
    return [(i, j) for i in range(count) for j in range(i, count)]


def folded_of(size):
    count = size // TILE
    return [(i, i + 1) for i in range(0, count, 2)], [(i, j) for i in range(count) for j in range(i + 1, count)]


def fold(gram, squares, devices):
    block = lambda i, j: gram[i * TILE : (i + 1) * TILE, j * TILE : (j + 1) * TILE]
    rows, lanes = (lax.broadcasted_iota(jnp.int32, (TILE, TILE), d) for d in (0, 1))
    pairs, above = folded_of(gram.shape[0])
    parts = [jnp.where(rows <= lanes, block(i, i), block(j, j)) for i, j in pairs]
    parts += [block(i, j) for i, j in above]
    parts += [squares[j * TILE : (j + 1) * TILE][None] for _, j in pairs]
    height = sum(part.shape[0] for part in parts)
    missing = -height % devices
    parts.append(jnp.zeros((missing, TILE), jnp.float32))
    return jnp.concatenate(parts, axis=0).reshape(devices, (height + missing) // devices, 1, TILE)


def exchange(value, axes):
    return lax.all_to_all(value, axes, split_axis=0, concat_axis=0, tiled=True)


def spread(value, axes):
    count = lax.axis_size(axes)
    return exchange(jnp.broadcast_to(value[None], (count,) + value.shape), axes)


def self_gram(matrix):
    high = lax.reduce_precision(matrix, 8, 7)
    rest = matrix - high
    middle = lax.reduce_precision(rest, 8, 7)
    low = rest - middle
    tall = jnp.concatenate([high, high, middle, middle, high, low]).astype(jnp.bfloat16)
    wide = jnp.concatenate([high, middle, high, middle, low, high]).astype(jnp.bfloat16)
    return lax.dot_general(tall, wide, (((0,), (0,)), ((), ())), preferred_element_type=jnp.float32)


def bucket_sums(design, scales, buckets, core, chips, owned):
    slots = lax.broadcasted_iota(jnp.int32, (chips, owned), 0) * (2 * owned) + core * owned
    slots = (slots + lax.broadcasted_iota(jnp.int32, (chips, owned), 1)).reshape(-1)
    table = jnp.where(slots[:, None] == buckets[None, :], scales[None, :], jnp.zeros((), jnp.bfloat16))
    return jnp.dot(table, design, preferred_element_type=jnp.float32)


def terms(value):
    high = value.astype(jnp.bfloat16).astype(jnp.float32)
    rest = value - high
    middle = rest.astype(jnp.bfloat16).astype(jnp.float32)
    return high, middle, rest - middle


def rank_update(left, right):
    a, b, c = terms(left)
    d, e, f = terms(right)
    tall = jnp.concatenate([a, a, b, b, a, c], 0).astype(jnp.bfloat16)
    wide = jnp.concatenate([d, e, d, e, f, d], 0).astype(jnp.bfloat16)
    return lax.dot_general(tall, wide, (((0,), (0,)), ((), ())), preferred_element_type=jnp.float32)


def fill(value):
    return jnp.broadcast_to(value, (SUB, TILE))


def pivots_of(rows, left):
    return {(t, u): fill(rows[t][:, left + u : left + u + 1]) for t in range(SUB) for u in range(t, SUB)}


def factor_kernel(slab_ref, gram_ref, out_ref, work, *, count, scale):
    at = {pair: n for n, pair in enumerate(blocks_of(count * TILE))}
    pairs, above = folded_of(count * TILE)
    shape = (TILE, TILE)
    rows, lanes = lax.broadcasted_iota(jnp.int32, shape, 0), lax.broadcasted_iota(jnp.int32, shape, 1)
    last = (len(pairs) + len(above)) * TILE
    for n, (i, j) in enumerate(pairs):
        both = gram_ref[n * TILE : (n + 1) * TILE, :]
        work[at[i, i]] = both
        diagonal = jnp.broadcast_to(gram_ref[last + n : last + n + 1, :], shape)
        work[at[j, j]] = jnp.where(rows == lanes, diagonal, both.T)
    for n, pair in enumerate(above, len(pairs)):
        work[at[pair]] = gram_ref[n * TILE : (n + 1) * TILE, :]
    for b in range(count):
        js = range(b, count)
        ahead = ready = None
        for top in range(0, TILE, SUB):
            rows, pivot = ahead, ready
            if rows is None:
                rows = [{j: fill(work[at[b, j], top + t : top + t + 1, :]) for j in js} for t in range(SUB)]
                pivot = pivots_of([row[b] for row in rows], top)
            done = []
            for t in range(SUB):
                inverse = lax.rsqrt(pivot[t, t])
                coef = {u: pivot[t, u] * inverse for u in range(t + 1, SUB)}
                for u in range(t + 1, SUB):
                    for v in range(u, SUB):
                        pivot[u, v] = pivot[u, v] - coef[u] * coef[v]
                done.append({j: rows[t][j] * inverse for j in js})
                for u in range(t + 1, SUB):
                    for j in js:
                        rows[u][j] = rows[u][j] - coef[u] * done[t][j]
            for t in range(SUB):
                for j in js:
                    work[at[b, j], top + t : top + t + 1, :] = done[t][j][0:1, :]
            ahead = ready = None
            below = top + SUB
            if below < TILE:
                ahead = [
                    {j: fill(work[at[b, j], below + u : below + u + 1, :]) for j in js} for u in range(SUB)
                ]
                for t in range(SUB):
                    if t == SUB // 2:
                        ready = pivots_of([row[b] for row in ahead], below)
                    coef = [fill(done[t][b][:, below + u : below + u + 1]) for u in range(SUB)]
                    if ready is not None:
                        for u, v in ready:
                            ready[u, v] = ready[u, v] - coef[u] * coef[v]
                    for u in range(SUB):
                        for j in js:
                            ahead[u][j] = ahead[u][j] - coef[u] * done[t][j]
            later = top + 2 * SUB
            if later < TILE:
                left = work[at[b, b], top : top + SUB, :]
                for j in js:
                    update = rank_update(left, work[at[b, j], top : top + SUB, :])
                    work[at[b, j], later:, :] = work[at[b, j], later:, :] - update[later:, :]
        for i in range(b + 1, count):
            for j in range(i, count):
                work[at[i, j]] = work[at[i, j]] - lax.dot_general(
                    work[at[b, i]],
                    work[at[b, j]],
                    (((0,), (0,)), ((), ())),
                    precision=lax.Precision.HIGHEST,
                    preferred_element_type=jnp.float32,
                )
    slab = slab_ref[0]
    height = out_ref.shape[0]
    per_tile = TILE // height
    for i in range(count):

        @pl.when(slab // per_tile == i)
        def _():
            start = pl.multiple_of((slab % per_tile) * height, height)
            shape = (height, TILE)
            for j in range(count):
                if j < i:
                    value = jnp.zeros(shape, jnp.float32)
                else:
                    value = work[at[i, j], pl.ds(start, height), :] * scale
                if j == i:
                    upper = lax.broadcasted_iota(jnp.int32, shape, 1) >= start + lax.broadcasted_iota(
                        jnp.int32, shape, 0
                    )
                    value = jnp.where(upper, value, 0.0)
                out_ref[:, j * TILE : (j + 1) * TILE] = value


def factor_rows(slab, packed, height, cols, scale):
    return pl.pallas_call(
        functools.partial(factor_kernel, count=cols // TILE, scale=scale),
        out_shape=jax.ShapeDtypeStruct((height, cols), jnp.float32),
        in_specs=[pl.BlockSpec(memory_space=pltpu.SMEM), pl.BlockSpec(memory_space=pltpu.VMEM)],
        out_specs=pl.BlockSpec(memory_space=pltpu.VMEM),
        scratch_shapes=[pltpu.VMEM((len(blocks_of(cols)), TILE, TILE), jnp.float32)],
        name="factor_rows",
    )(slab.reshape(1), pltpu.with_memory_space_constraint(packed, pltpu.VMEM))


def per_device(design, scales, buckets):
    rows, cols = design.shape
    chips = lax.axis_size(("x", "y"))
    owned = rows // (2 * chips)
    core = lax.axis_index("core")
    slab = lax.axis_index(("zh", "zl")).astype(jnp.int32)
    core, slab, buckets = lax.optimization_barrier((core, slab, buckets))
    theirs = bucket_sums(design, scales, buckets, 1 - core, chips, owned)
    from_pair = lax.ppermute(theirs, "core", [(0, 1), (1, 0)])
    ours = lax.optimization_barrier(bucket_sums(design, scales, buckets, core, chips, owned))
    paired = (ours + from_pair).reshape(chips, owned, cols)
    sketch = jnp.sum(exchange(paired, ("x", "y")), axis=0)
    local = self_gram(sketch)
    packed = fold(local, jnp.sum(sketch * sketch, axis=0), 2 * chips)
    piece = jnp.sum(exchange(packed, ("x", "y", "core")), axis=0)
    piece = jnp.sum(spread(piece, ("zh",)), axis=0)
    piece = jnp.sum(spread(piece, ("zl",)), axis=0)
    whole = spread(piece, ("x", "y", "core")).reshape(-1, TILE)
    groups = lax.axis_size(("zh", "zl"))
    precond = factor_rows(slab, whole, cols // groups, cols, 1.0 / math.sqrt(rows * groups))
    return sketch, precond


def solution(mesh):
    fine = Mesh(mesh.devices.reshape(4, 4, 4, 4, 2), ALL)
    rows = ALL
    in_specs = (P(rows, None), P(rows), P(rows))
    out_specs = (P(rows, None), P(("zh", "zl"), None))
    return jax.shard_map(
        per_device, mesh=fine, in_specs=in_specs, out_specs=out_specs, check_vma=False
    )
```

```python
import functools
import math

import jax
import jax.numpy as jnp
from jax import lax
from jax.experimental import pallas as pl
from jax.experimental.pallas import tpu as pltpu
from jax.sharding import Mesh
from jax.sharding import PartitionSpec as P

TILE = 128
SUB = 8
ALL = ("zh", "zl", "x", "y", "core")


def blocks_of(size):
    count = size // TILE
    return [(i, j) for i in range(count) for j in range(i, count)]


def folded_of(size):
    count = size // TILE
    return [(i, i + 1) for i in range(0, count, 2)], [(i, j) for i in range(count) for j in range(i + 1, count)]


def fold(gram, squares, devices):
    block = lambda i, j: gram[i * TILE : (i + 1) * TILE, j * TILE : (j + 1) * TILE]
    rows, lanes = (lax.broadcasted_iota(jnp.int32, (TILE, TILE), d) for d in (0, 1))
    pairs, above = folded_of(gram.shape[0])
    parts = [jnp.where(rows <= lanes, block(i, i), block(j, j)) for i, j in pairs]
    parts += [block(i, j) for i, j in above]
    parts += [squares[j * TILE : (j + 1) * TILE][None] for _, j in pairs]
    height = sum(part.shape[0] for part in parts)
    missing = -height % devices
    parts.append(jnp.zeros((missing, TILE), jnp.float32))
    return jnp.concatenate(parts, axis=0).reshape(devices, (height + missing) // devices, 1, TILE)


def exchange(value, axes):
    return lax.all_to_all(value, axes, split_axis=0, concat_axis=0, tiled=True)


def spread(value, axes):
    count = lax.axis_size(axes)
    return exchange(jnp.broadcast_to(value[None], (count,) + value.shape), axes)


def self_gram(matrix):
    high = lax.reduce_precision(matrix, 8, 7)
    rest = matrix - high
    middle = lax.reduce_precision(rest, 8, 7)
    low = rest - middle
    tall = jnp.concatenate([high, high, middle, middle, high, low]).astype(jnp.bfloat16)
    wide = jnp.concatenate([high, middle, high, middle, low, high]).astype(jnp.bfloat16)
    return lax.dot_general(tall, wide, (((0,), (0,)), ((), ())), preferred_element_type=jnp.float32)


def bucket_sums(design, scales, buckets, core, chips, owned):
    slots = lax.broadcasted_iota(jnp.int32, (chips, owned), 0) * (2 * owned) + core * owned
    slots = (slots + lax.broadcasted_iota(jnp.int32, (chips, owned), 1)).reshape(-1)
    table = jnp.where(slots[:, None] == buckets[None, :], scales[None, :], jnp.zeros((), jnp.bfloat16))
    return jnp.dot(table, design, preferred_element_type=jnp.float32)


def terms(value):
    high = value.astype(jnp.bfloat16).astype(jnp.float32)
    rest = value - high
    middle = rest.astype(jnp.bfloat16).astype(jnp.float32)
    return high, middle, rest - middle


def rank_update(left, right):
    a, b, c = terms(left)
    d, e, f = terms(right)
    tall = jnp.concatenate([a, a, b, b, a, c], 0).astype(jnp.bfloat16)
    wide = jnp.concatenate([d, e, d, e, f, d], 0).astype(jnp.bfloat16)
    return lax.dot_general(tall, wide, (((0,), (0,)), ((), ())), preferred_element_type=jnp.float32)


def fill(value):
    return jnp.broadcast_to(value, (SUB, TILE))


def pivots_of(rows, left):
    return {(t, u): fill(rows[t][:, left + u : left + u + 1]) for t in range(SUB) for u in range(t, SUB)}


def factor_kernel(slab_ref, gram_ref, out_ref, work, *, count, scale):
    at = {pair: n for n, pair in enumerate(blocks_of(count * TILE))}
    pairs, above = folded_of(count * TILE)
    shape = (TILE, TILE)
    rows, lanes = lax.broadcasted_iota(jnp.int32, shape, 0), lax.broadcasted_iota(jnp.int32, shape, 1)
    last = (len(pairs) + len(above)) * TILE
    for n, (i, j) in enumerate(pairs):
        both = gram_ref[n * TILE : (n + 1) * TILE, :]
        work[at[i, i]] = both
        diagonal = jnp.broadcast_to(gram_ref[last + n : last + n + 1, :], shape)
        work[at[j, j]] = jnp.where(rows == lanes, diagonal, both.T)
    for n, pair in enumerate(above, len(pairs)):
        work[at[pair]] = gram_ref[n * TILE : (n + 1) * TILE, :]
    for b in range(count):
        js = range(b, count)
        ahead = ready = None
        for top in range(0, TILE, SUB):
            rows, pivot = ahead, ready
            if rows is None:
                rows = [{j: fill(work[at[b, j], top + t : top + t + 1, :]) for j in js} for t in range(SUB)]
                pivot = pivots_of([row[b] for row in rows], top)
            done = []
            for t in range(SUB):
                inverse = lax.rsqrt(pivot[t, t])
                coef = {u: pivot[t, u] * inverse for u in range(t + 1, SUB)}
                for u in range(t + 1, SUB):
                    for v in range(u, SUB):
                        pivot[u, v] = pivot[u, v] - coef[u] * coef[v]
                done.append({j: rows[t][j] * inverse for j in js})
                for u in range(t + 1, SUB):
                    for j in js:
                        rows[u][j] = rows[u][j] - coef[u] * done[t][j]
            for t in range(SUB):
                for j in js:
                    work[at[b, j], top + t : top + t + 1, :] = done[t][j][0:1, :]
            ahead = ready = None
            below = top + SUB
            if below < TILE:
                ahead = [
                    {j: fill(work[at[b, j], below + u : below + u + 1, :]) for j in js} for u in range(SUB)
                ]
                for t in range(SUB):
                    if t == SUB // 2:
                        ready = pivots_of([row[b] for row in ahead], below)
                    coef = [fill(done[t][b][:, below + u : below + u + 1]) for u in range(SUB)]
                    if ready is not None:
                        for u, v in ready:
                            ready[u, v] = ready[u, v] - coef[u] * coef[v]
                    for u in range(SUB):
                        for j in js:
                            ahead[u][j] = ahead[u][j] - coef[u] * done[t][j]
            later = top + 2 * SUB
            if later < TILE:
                left = work[at[b, b], top : top + SUB, :]
                for j in js:
                    update = rank_update(left, work[at[b, j], top : top + SUB, :])
                    work[at[b, j], later:, :] = work[at[b, j], later:, :] - update[later:, :]
        for i in range(b + 1, count):
            for j in range(i, count):
                work[at[i, j]] = work[at[i, j]] - rank_update(work[at[b, i]], work[at[b, j]])
    slab = slab_ref[0]
    height = out_ref.shape[0]
    per_tile = TILE // height
    for i in range(count):

        @pl.when(slab // per_tile == i)
        def _():
            start = pl.multiple_of((slab % per_tile) * height, height)
            shape = (height, TILE)
            for j in range(count):
                if j < i:
                    value = jnp.zeros(shape, jnp.float32)
                else:
                    value = work[at[i, j], pl.ds(start, height), :] * scale
                if j == i:
                    upper = lax.broadcasted_iota(jnp.int32, shape, 1) >= start + lax.broadcasted_iota(
                        jnp.int32, shape, 0
                    )
                    value = jnp.where(upper, value, 0.0)
                out_ref[:, j * TILE : (j + 1) * TILE] = value


def factor_rows(slab, packed, height, cols, scale):
    return pl.pallas_call(
        functools.partial(factor_kernel, count=cols // TILE, scale=scale),
        out_shape=jax.ShapeDtypeStruct((height, cols), jnp.float32),
        in_specs=[pl.BlockSpec(memory_space=pltpu.SMEM), pl.BlockSpec(memory_space=pltpu.VMEM)],
        out_specs=pl.BlockSpec(memory_space=pltpu.VMEM),
        scratch_shapes=[pltpu.VMEM((len(blocks_of(cols)), TILE, TILE), jnp.float32)],
        name="factor_rows",
    )(slab.reshape(1), pltpu.with_memory_space_constraint(packed, pltpu.VMEM))


def per_device(design, scales, buckets):
    rows, cols = design.shape
    chips = lax.axis_size(("x", "y"))
    owned = rows // (2 * chips)
    core = lax.axis_index("core")
    slab = lax.axis_index(("zh", "zl")).astype(jnp.int32)
    core, slab, buckets = lax.optimization_barrier((core, slab, buckets))
    theirs = bucket_sums(design, scales, buckets, 1 - core, chips, owned)
    from_pair = lax.ppermute(theirs, "core", [(0, 1), (1, 0)])
    ours = lax.optimization_barrier(bucket_sums(design, scales, buckets, core, chips, owned))
    paired = (ours + from_pair).reshape(chips, owned, cols)
    sketch = jnp.sum(exchange(paired, ("x", "y")), axis=0)
    local = self_gram(sketch)
    packed = fold(local, jnp.sum(sketch * sketch, axis=0), 2 * chips)
    piece = jnp.sum(exchange(packed, ("x", "y", "core")), axis=0)
    piece = jnp.sum(spread(piece, ("zh",)), axis=0)
    piece = jnp.sum(spread(piece, ("zl",)), axis=0)
    whole = spread(piece, ("x", "y", "core")).reshape(-1, TILE)
    groups = lax.axis_size(("zh", "zl"))
    precond = factor_rows(slab, whole, cols // groups, cols, 1.0 / math.sqrt(rows * groups))
    return sketch, precond


def solution(mesh):
    fine = Mesh(mesh.devices.reshape(4, 4, 4, 4, 2), ALL)
    rows = ALL
    in_specs = (P(rows, None), P(rows), P(rows))
    out_specs = (P(rows, None), P(("zh", "zl"), None))
    return jax.shard_map(
        per_device, mesh=fine, in_specs=in_specs, out_specs=out_specs, check_vma=False
    )
```
